32 devices in a mesh: groups: 2 (over x), expert: 16 (over z, y, core).
Axes of the slice: x: 2, y: 2, z: 4, core: 2. Of those that a mesh axis runs over, the one named last changes fastest.
Arguments:
- hidden_states: bfloat16 [2, 1024, 2560], P(None, ('groups', 'expert')), parts along dimension 1, may hold values from -6 to 6
- route_ids: int32 [2, 1024, 8], P(None, ('groups', 'expert')), parts along dimension 1, may hold values from 0 to 15, all different within a row; in each aligned block of 32 rows (0 to 31, 32 to 63, ..., all dimensions but the last counted through in order) at most 24 rows name the same one
- route_weights: float32 [2, 1024, 8], P(None, ('groups', 'expert')), parts along dimension 1, may hold values from 0.05 to 1
- gate_proj: bfloat16 [16, 2560, 768], P('expert'), may hold values from -0.125 to 0.125
- up_proj: bfloat16 [16, 2560, 768], P('expert'), may hold values from -0.125 to 0.125
- down_proj: bfloat16 [16, 768, 2560], P('expert'), may hold values from -0.21875 to 0.21875
Outputs:
- moe_output: bfloat16 [2, 1024, 2560], P(None, ('groups', 'expert')), parts along dimension 1
The draws below stay inside these ranges and needn't reach their ends.
There are 2 independent parts, one for each index of `groups`. The reference program is written for one: setup_inputs(seed, part) draws one part's arguments, and reference() takes and returns one part's arrays. A program takes and returns all parts, laid end to end along the dimension named above; an argument that names none is the same for every part. Nothing has to cross between parts.
Inputs may be any that keep to these rules, and one draw needn't show every extreme that they name: `route_ids`: each row names 8 different experts. In each micro-batch, the 32 rows of one device name one expert at most 24 times, and some device names some expert exactly 24 times.
All inputs are finite; a program needn't handle non-finite values.
Results may differ from the reference program's by a relative error of at most 0.0057.
Values may be sent and summed in bfloat16 or wider, within the bound.
A program may use at most 64 MiB of HBM per device.

```python
import math
import jax
import jax.numpy as jnp
import numpy as np
from jax import lax

D = 2560
FF = 768
TOPK = 8
STEPS = 2
ROWS = 32
EXPERTS = 16
TOKENS = 512
CAP = 24
N_EXPERT = 16


def level_of(own_key, dims, cuts, smallest, largest):
    def one(dim, parts):
        heights = jax.random.uniform(jax.random.fold_in(jax.random.fold_in(own_key, 6), dim), (parts,), jnp.float32, smallest / len(cuts), largest / len(cuts))
        return jnp.repeat(jnp.exp(heights), dims[dim] // parts).reshape((-1,) + (1,) * (len(dims) - dim - 1))

    factor_of = one(*cuts[0])
    for cut in cuts[1:]:
        factor_of = factor_of * one(*cut)
    return factor_of


def routed_block(key, own, number, rows, amount, top, limit, lean):
    sequence = jax.random.permutation(key, amount)
    packed, ordinary = shares(amount, rows * top, limit, lean, True), shares(amount, rows * top, limit, lean, False)
    places = jnp.arange(amount)

    def named(tallies, offset_by):
        used = int((tallies > 0).sum())
        fixed = max(1, used // 4)
        shifted = fixed + (places - fixed + offset_by * (used - fixed)) % max(1, amount - fixed)
        return jnp.zeros((amount,), jnp.int32).at[sequence[jnp.where(places < fixed, places, shifted)]].set(jnp.asarray(tallies, jnp.int32))

    tallies = jnp.where(number % 4 == 0, named(packed, number // 4), named(ordinary, number - number // 4 - 1))
    mixed = jax.random.permutation(jax.random.fold_in(own, 3), amount)
    donor, receiver = mixed[0:amount // 2 * 2:2], mixed[1:amount // 2 * 2:2]
    room = jnp.minimum(tallies[donor] - 1, limit - tallies[receiver]) // 2
    room = jnp.where((donor == sequence[0]) | (receiver == sequence[0]) | (tallies[receiver] == 0), 0, jnp.maximum(room, 0))
    shifted = jax.random.randint(jax.random.fold_in(own, 4), (amount // 2,), 0, 1 << 20) % (room + 1)
    tallies = tallies.at[donor].add(-shifted).at[receiver].add(shifted)
    items = jnp.searchsorted(jnp.cumsum(tallies), jnp.arange(rows * top), side="right").astype(jnp.int32)
    table = items.reshape(top, rows).T
    table = table[jax.random.permutation(jax.random.fold_in(own, 1), rows)]
    offset_by = jax.random.randint(jax.random.fold_in(own, 2), (rows, 1), 0, top)
    return jnp.take_along_axis(table, (jnp.arange(top)[None, :] + offset_by) % top, axis=1)


def shares(number_of, total, limit, skew, full):
    portions = [(1 << 20) // math.isqrt(standing ** skew) + 1 for standing in range(1, number_of + 1)]
    largest = limit if full else min(limit, max(-(-total // number_of), total * portions[0] // sum(portions)))
    least = 1 if total - largest >= number_of - 1 else 0
    given, rest = [largest] + [least] * (number_of - 1), total - largest - least * (number_of - 1)
    while rest > 0:
        candidates = [i for i in range(1, number_of) if given[i] < largest] or [i for i in range(1, number_of) if given[i] < limit]
        pool, left = sum([portions[i] for i in candidates]), rest
        for i in candidates:
            extra = min(limit - given[i], max(1, left * portions[i] // pool), rest)
            given[i] = given[i] + extra
            rest = rest - extra
    return np.array(given)


def scatter_about(rng, extent, deviation, most, split=(), dtype=jnp.bfloat16):
    entries = deviation * jax.random.normal(rng, extent, jnp.float32)
    if split:
        entries = entries * level_of(rng, extent, split, -0.22, 0.18)
    return jnp.clip(entries, -most, most).astype(dtype)


def setup_inputs(seed: int = 0, part: int = 0) -> dict:
    keys = jax.random.split(jax.random.key(seed), 7)
    part_keys = jax.random.split(jax.random.fold_in(keys[6], part), 7)
    hidden_states = scatter_about(part_keys[0], (STEPS, TOKENS, D), 1.0, 6.0, ((1, 16),))
    route_ids_keys = jax.random.split(jax.random.fold_in(part_keys[1], 1), STEPS * TOKENS // ROWS)
    route_ids_turns = jax.random.permutation(jax.random.fold_in(part_keys[1], 3), STEPS * TOKENS // ROWS)
    route_ids = jax.vmap(lambda own, number: routed_block(jax.random.fold_in(part_keys[1], 2), own, number, ROWS, EXPERTS, TOPK, CAP, 2))(route_ids_keys, route_ids_turns).reshape((STEPS, TOKENS, TOPK))
    route_weights = jnp.clip(0.05 + 0.95 * jax.random.uniform(part_keys[2], (STEPS, TOKENS, TOPK), jnp.float32) ** level_of(part_keys[2], (STEPS, TOKENS, TOPK), ((1, 16),), -0.2, 0.2), 0.05, 1.0)
    gate_proj = scatter_about(keys[3], (EXPERTS, D, FF), D ** -0.5, 0.125, ((0, 16),))
    up_proj = scatter_about(keys[4], (EXPERTS, D, FF), D ** -0.5, 0.125, ((0, 16),))
    down_proj = scatter_about(keys[5], (EXPERTS, FF, D), FF ** -0.5, 0.21875, ((0, 16),))
    return dict(hidden_states=hidden_states, route_ids=route_ids, route_weights=route_weights, gate_proj=gate_proj, up_proj=up_proj, down_proj=down_proj)


def slot_targets(route_row, capacity):
    labels = lax.broadcasted_iota(jnp.int32, (TOKENS, TOPK, EXPERTS), 2)
    onehot = (route_row[:, :, None] == labels).astype(jnp.int32)
    per_row = jnp.sum(onehot, axis=1)
    before = jnp.cumsum(per_row, axis=0) - per_row
    position = jnp.sum(onehot * before[:, None, :], axis=2)
    return (route_row * capacity + position).astype(jnp.int32)


def apply_expert(operands):
    expert_rows, gate_weight, up_weight, down_weight = operands
    gate_values = jnp.dot(expert_rows, gate_weight, preferred_element_type=jnp.float32)
    up_values = jnp.dot(expert_rows, up_weight, preferred_element_type=jnp.float32)
    hidden = (jax.nn.silu(gate_values) * up_values).astype(jnp.bfloat16)
    return jnp.dot(hidden, down_weight, preferred_element_type=jnp.float32).astype(jnp.bfloat16)


def reference(hidden_states, route_ids, route_weights, gate_proj, up_proj, down_proj):
    capacity = N_EXPERT * CAP
    outputs = []
    for step_index in range(STEPS):
        targets = slot_targets(route_ids[step_index], capacity).reshape(-1)
        sources = jnp.repeat(hidden_states[step_index], TOPK, axis=0)
        buffer = jnp.zeros((EXPERTS * capacity, D), jnp.bfloat16).at[targets].set(sources)
        results = lax.map(apply_expert, (buffer.reshape(EXPERTS, capacity, D), gate_proj, up_proj, down_proj))
        gathered = results.reshape(EXPERTS * capacity, D)[targets].reshape(TOKENS, TOPK, D)
        weights = route_weights[step_index]
        normalized = weights / jnp.sum(weights, axis=1, keepdims=True)
        combined = jnp.sum(gathered.astype(jnp.float32) * normalized[:, :, None], axis=1)
        outputs.append(combined.astype(jnp.bfloat16))
    return jnp.stack(outputs)
```

```python
import jax
import jax.numpy as jnp
from jax import lax
from jax.sharding import PartitionSpec as P


def on_device(hidden_states, route_ids, route_weights, gate_proj, up_proj, down_proj):
    step_count, row_count, feature_width = hidden_states.shape
    experts = lax.axis_size("expert")
    me = lax.axis_index("expert")
    normalized = route_weights / jnp.sum(route_weights, axis=2, keepdims=True)
    labels = lax.broadcasted_iota(jnp.int32, (1, 1, 1, experts), 3)
    dense = jnp.sum(
        jnp.where(route_ids[:, :, :, None] == labels, normalized[:, :, :, None], 0.0), axis=2
    )
    all_dense = lax.all_gather(dense, "expert", axis=1, tiled=True)
    mine = jnp.sum(
        jnp.where(lax.broadcasted_iota(jnp.int32, (1, 1, experts), 2) == me, all_dense, 0.0),
        axis=2,
    )
    outputs = []
    for step in range(step_count):
        tokens = lax.all_gather(hidden_states[step], "expert", axis=0, tiled=True)
        gate_values = jnp.dot(tokens, gate_proj[0], preferred_element_type=jnp.float32)
        up_values = jnp.dot(tokens, up_proj[0], preferred_element_type=jnp.float32)
        hidden = (jax.nn.silu(gate_values) * up_values).astype(jnp.bfloat16)
        result = jnp.dot(hidden, down_proj[0], preferred_element_type=jnp.float32)
        partial = (result * mine[step][:, None]).astype(jnp.bfloat16)
        outputs.append(lax.psum_scatter(partial, "expert", scatter_dimension=0, tiled=True))
    return jnp.stack(outputs)


def solution(mesh):
    placed = (
        P(None, ("groups", "expert"), None),
        P(None, ("groups", "expert"), None),
        P(None, ("groups", "expert"), None),
        P("expert", None, None),
        P("expert", None, None),
        P("expert", None, None),
    )
    return jax.shard_map(
        on_device,
        mesh=mesh,
        in_specs=placed,
        out_specs=P(None, ("groups", "expert"), None),
        check_vma=False,
    )
```

```python
import functools

import jax
import jax.numpy as jnp
from jax import lax
from jax.experimental import pallas as pl
from jax.experimental.pallas import tpu as pltpu
from jax.sharding import PartitionSpec as P

MESH = pl.DeviceIdType.MESH
LANES = 128


def kernel(
    chips,
    across,
    hidden_ref,
    ids_ref,
    weights_ref,
    gate_hbm,
    up_hbm,
    down_hbm,
    out_ref,
    x,
    pc,
    rs,
    gate,
    up,
    down,
    mid,
    load_sem,
    ag_s,
    ag_r,
    pf_s,
    pf_r,
    pc_s,
    pc_r,
    rs_s,
    rs_r,
):
    steps, _, _, rows, _ = x.shape
    width = out_ref.shape[2]
    inner = gate.shape[1]
    experts = 2 * chips
    hops = (chips // 2, chips - 1 - chips // 2)
    along = chips // across

    me = lax.axis_index("expert")
    core = lax.rem(me, 2)
    chip = lax.div(me, 2)
    if across == 2:
        far, deep = lax.rem(chip, 2), lax.div(chip, 2)
        here = (1 - far) * deep + far * (2 * along - 1 - deep)
    else:
        here = chip

    def device_at(position):
        if across == 2:
            far = lax.div(position, along)
            deep = (1 - far) * position + far * (2 * along - 1 - position)
            position = deep * 2 + far
        return {"expert": position * 2 + core}

    sign = 1 - 2 * core
    neighbours = (
        device_at(lax.rem(here + sign + chips, chips)),
        device_at(lax.rem(here - sign + chips, chips)),
    )
    partner = {"expert": chip * 2 + (1 - core)}

    def slot(direction, hop):
        return hop if direction == 0 else (chips - hop) % chips

    order = [0]
    for hop in range(1, chips // 2 + 1):
        order += [slot(d, hop) for d in range(2) if hop <= hops[d]]
    place = {s: i for i, s in enumerate(order)}
    values = pl.ds(0, width)

    def remote(src, dst, send, recv, target):
        return pltpu.make_async_remote_copy(
            src_ref=src,
            dst_ref=dst,
            send_sem=send,
            recv_sem=recv,
            device_id=target,
            device_id_type=MESH,
        )

    def mirror(s):
        return (chips - s) % chips

    def ag_copy(st, d, hop):
        return remote(
            x.at[st, place[slot(d, hop - 1)], 0],
            x.at[st, place[slot(d, hop)], 0],
            ag_s.at[st, d, hop - 1],
            ag_r.at[st, d, hop - 1],
            neighbours[d],
        )

    def pf_copy(st, s):
        return remote(
            x.at[st, place[s], 0],
            x.at[st, place[mirror(s)], 1],
            pf_s.at[st, s],
            pf_r.at[st, mirror(s)],
            partner,
        )

    def pc_copy(st, s):
        return remote(
            x.at[st, place[s], 1, :, values],
            pc.at[st, mirror(s)],
            pc_s.at[st, s],
            pc_r.at[st, mirror(s)],
            partner,
        )

    def rs_copy(st, d, hop):
        target = slot(d, hop - 1) if (d == 0 or hop > 1) else chips // 2
        return remote(
            x.at[st, place[slot(d, hop)], 0, :, values],
            rs.at[st, target],
            rs_s.at[st, d, hop - 1],
            rs_r.at[st, d, hop - 1],
            neighbours[1 - d],
        )

    own = [
        pltpu.make_async_copy(
            hidden_ref.at[st], x.at[st, 0, 0, :, values], load_sem.at[3 + st]
        )
        for st in range(steps)
    ]
    for copy in own:
        copy.start()
    loads = [
        pltpu.make_async_copy(src.at[0], dst, load_sem.at[i])
        for i, (src, dst) in enumerate(((gate_hbm, gate), (up_hbm, up), (down_hbm, down)))
    ]
    for copy in loads:
        copy.start()

    barrier = pltpu.get_barrier_semaphore()
    for target in (*neighbours, partner):
        pl.semaphore_signal(barrier, inc=1, device_id=target, device_id_type=MESH)

    extra = x.shape[4] - width
    lane = lax.broadcasted_iota(jnp.int32, (rows, extra), 1)
    for st in range(steps):
        raw = weights_ref[st]
        normalized = raw / jnp.sum(raw, axis=1, keepdims=True)
        ids = ids_ref[st]
        dense = jnp.zeros((rows, extra), jnp.float32)
        for k in range(ids.shape[1]):
            label = ids[:, k : k + 1]
            hit = (lane == label) | (lane == label + experts)
            dense = dense + jnp.where(hit, normalized[:, k : k + 1], 0.0)
        high = dense.astype(jnp.bfloat16).astype(jnp.float32)
        low = dense - high
        x[st, 0, 0, :, pl.ds(width, extra)] = jnp.where(lane < experts, high, low).astype(
            jnp.bfloat16
        )
    pl.semaphore_wait(barrier, 3)

    def ag_open(st):
        own[st].wait()
        for d in range(2):
            ag_copy(st, d, 1).start()
        pf_copy(st, 0).start()

    def ag_event(st, hop):
        for d in range(2):
            if hop <= hops[d]:
                ag_copy(st, d, hop).wait_recv()
                if hop < hops[d]:
                    ag_copy(st, d, hop + 1).start()
                pf_copy(st, slot(d, hop)).start()

    def total(st, s, received):
        value = x[st, place[s], 0, :, values].astype(jnp.float32)
        value = value + pc[st, s].astype(jnp.float32)
        for index in received:
            value = value + rs[st, index].astype(jnp.float32)
        return value.astype(jnp.bfloat16)

    def rs_event(st, hop):
        for d in range(2):
            if hop <= hops[d]:
                s = slot(d, hop)
                received = []
                if hop < hops[d]:
                    rs_copy(st, d, hop + 1).wait_recv()
                    received = [s]
                pc_copy(st, mirror(s)).wait_recv()
                x[st, place[s], 0, :, values] = total(st, s, received)
                rs_copy(st, d, hop).start()

    def rs_close(st):
        for d in range(2):
            rs_copy(st, d, 1).wait_recv()
        pc_copy(st, 0).wait_recv()
        out_ref[st] = total(st, 0, [0, chips // 2])

    group = chips // 2
    block = min(4, group)
    tall = block * 2 * rows
    ff_tile = 256 if inner % 256 == 0 else inner
    out_tile = 512 if width % 512 == 0 else width

    def over_blocks(first, body):
        if group == block:
            body(first, 0)
        else:
            def step(i, carry):
                body(first + i * block, i * tall)
                return carry

            lax.fori_loop(0, group // block, step, 0)

    def gate_up(st, part, tile):
        columns = pl.ds(tile * ff_tile, ff_tile)

        def body(first, row):
            rows_in = x[st, pl.ds(first, block), :, :, values].reshape(tall, width)
            g = jnp.dot(rows_in, gate[:, columns], preferred_element_type=jnp.float32)
            u = jnp.dot(rows_in, up[:, columns], preferred_element_type=jnp.float32)
            mid[pl.ds(row, tall), columns] = (g / (1.0 + jnp.exp(-g)) * u).astype(jnp.bfloat16)

        over_blocks(part * group, body)

    def down_all(st, part):
        for s in order[part * group : (part + 1) * group]:
            pf_copy(st, s).wait_send()
            for d in range(2):
                for hop in range(hops[d]):
                    if slot(d, hop) == s:
                        ag_copy(st, d, hop + 1).wait_send()

        def body(first, row):
            marks = x[st, pl.ds(first, block), :, :, pl.ds(width, extra)].reshape(tall, extra)
            spot = lax.broadcasted_iota(jnp.int32, (tall, extra), 1)
            picked = (spot == me) | (spot == me + experts)
            scale = jnp.sum(
                jnp.where(picked, marks.astype(jnp.float32), 0.0), axis=1, keepdims=True
            )
            rows_in = mid[pl.ds(row, tall), :]

            def tile(i, carry):
                columns = pl.ds(pl.multiple_of(i * out_tile, out_tile), out_tile)
                y = jnp.dot(rows_in, down[:, columns], preferred_element_type=jnp.float32)
                y = (y * scale).astype(jnp.bfloat16).reshape(block, 2, rows, out_tile)
                x[st, pl.ds(first, block), :, :, columns] = y
                return carry

            lax.fori_loop(0, width // out_tile, tile, 0)

        over_blocks(part * group, body)
        for s in order[part * group : (part + 1) * group]:
            pc_copy(st, s).start()

    def arrive(st, part):
        for s in order[part * group : (part + 1) * group]:
            pf_copy(st, mirror(s)).wait_recv()

    def compute(st, part, events):
        tiles = inner // ff_tile
        pieces = tiles + 1
        arrive(st, part)
        taken = 0
        for piece in range(pieces):
            if piece < tiles:
                gate_up(st, part, piece)
            else:
                down_all(st, part)
            until = (piece + 1) * len(events) // pieces
            for event in events[taken:until]:
                event()
            taken = until

    near = group // 2
    call = functools.partial
    ag_open(0)
    for hop in range(1, near + 1):
        ag_event(0, hop)
    for copy in loads:
        copy.wait()
    rest = [call(ag_event, 0, hop) for hop in range(near + 1, hops[0] + 1)]
    compute(0, 0, rest + [call(ag_open, 1)])
    later = [call(ag_event, 1, hop) for hop in range(1, hops[0] + 1)]
    compute(0, 1, later[:near])
    back = [call(rs_event, 0, hop) for hop in range(hops[0], 0, -1)]
    mixed = []
    for i in range(near):
        mixed += [back[i]] + later[near + i * (len(later) - near) // near : near + (i + 1) * (len(later) - near) // near]
    compute(1, 0, mixed)
    compute(1, 1, back[near:] + [call(rs_close, 0)])
    for hop in range(hops[0], 0, -1):
        rs_event(1, hop)
    rs_close(1)

    for st in range(steps):
        for d in range(2):
            for hop in range(1, hops[d] + 1):
                rs_copy(st, d, hop).wait_send()
        for s in range(chips):
            pc_copy(st, s).wait_send()


def on_device(across, hidden_states, route_ids, route_weights, gate_proj, up_proj, down_proj):
    steps, rows, width = hidden_states.shape
    experts = lax.axis_size("expert")
    inner = gate_proj.shape[2]
    chips = experts // 2
    hops = chips // 2
    extra = -(-2 * experts // LANES) * LANES
    dma = pltpu.SemaphoreType.DMA
    bf16 = jnp.bfloat16
    vmem = pl.BlockSpec(memory_space=pltpu.VMEM)
    hbm = pl.BlockSpec(memory_space=pl.ANY)
    return pl.pallas_call(
        functools.partial(kernel, chips, across),
        out_shape=jax.ShapeDtypeStruct((steps, rows, width), bf16),
        in_specs=[hbm, vmem, vmem, hbm, hbm, hbm],
        out_specs=vmem,
        scratch_shapes=[
            pltpu.VMEM((steps, chips, 2, rows, width + extra), bf16),
            pltpu.VMEM((steps, chips, rows, width), bf16),
            pltpu.VMEM((steps, chips, rows, width), bf16),
            pltpu.VMEM((width, inner), bf16),
            pltpu.VMEM((width, inner), bf16),
            pltpu.VMEM((inner, width), bf16),
            pltpu.VMEM((chips * rows, inner), bf16),
            dma((3 + steps,)),
            dma((steps, 2, hops)),
            dma((steps, 2, hops)),
            dma((steps, chips)),
            dma((steps, chips)),
            dma((steps, chips)),
            dma((steps, chips)),
            dma((steps, 2, hops)),
            dma((steps, 2, hops)),
        ],
        compiler_params=pltpu.CompilerParams(
            collective_id=0, has_side_effects=True, vmem_limit_bytes=64_000_000
        ),
    )(hidden_states, route_ids, route_weights, gate_proj, up_proj, down_proj)


def solution(mesh):
    across = 2 if mesh.shape["groups"] == 2 else 1
    placed = (
        P(None, ("groups", "expert"), None),
        P(None, ("groups", "expert"), None),
        P(None, ("groups", "expert"), None),
        P("expert", None, None),
        P("expert", None, None),
        P("expert", None, None),
    )
    return jax.shard_map(
        functools.partial(on_device, across),
        mesh=mesh,
        in_specs=placed,
        out_specs=P(None, ("groups", "expert"), None),
        check_vma=False,
    )
```

```python
import functools

import jax
import jax.numpy as jnp
from jax import lax
from jax.experimental import pallas as pl
from jax.experimental.pallas import tpu as pltpu
from jax.sharding import PartitionSpec as P

MESH = pl.DeviceIdType.MESH
LANES = 128
CUTS = 2


def kernel(
    chips,
    across,
    hidden_ref,
    ids_ref,
    weights_ref,
    gate_hbm,
    up_hbm,
    down_hbm,
    out_ref,
    x,
    pc,
    rs,
    gate,
    up,
    down,
    mid,
    load_sem,
    ag_s,
    ag_r,
    pf_s,
    pf_r,
    pc_s,
    pc_r,
    rs_s,
    rs_r,
):
    steps, _, _, rows, _ = x.shape
    width = out_ref.shape[2]
    inner = gate.shape[1]
    experts = 2 * chips
    hops = (chips // 2, chips - 1 - chips // 2)
    along = chips // across

    me = lax.axis_index("expert")
    core = lax.rem(me, 2)
    chip = lax.div(me, 2)
    if across == 2:
        far, deep = lax.rem(chip, 2), lax.div(chip, 2)
        here = (1 - far) * deep + far * (2 * along - 1 - deep)
    else:
        here = chip

    def device_at(position):
        if across == 2:
            far = lax.div(position, along)
            deep = (1 - far) * position + far * (2 * along - 1 - position)
            position = deep * 2 + far
        return {"expert": position * 2 + core}

    sign = 1 - 2 * core
    neighbours = (
        device_at(lax.rem(here + sign + chips, chips)),
        device_at(lax.rem(here - sign + chips, chips)),
    )
    partner = {"expert": chip * 2 + (1 - core)}

    def slot(direction, hop):
        return hop if direction == 0 else (chips - hop) % chips

    order = [0]
    for hop in range(1, chips // 2 + 1):
        order += [slot(d, hop) for d in range(2) if hop <= hops[d]]
    place = {s: i for i, s in enumerate(order)}
    values = pl.ds(0, width)
    cut = rows // CUTS

    def some(q):
        return pl.ds(q * cut, cut)

    def remote(src, dst, send, recv, target):
        return pltpu.make_async_remote_copy(
            src_ref=src,
            dst_ref=dst,
            send_sem=send,
            recv_sem=recv,
            device_id=target,
            device_id_type=MESH,
        )

    def mirror(s):
        return (chips - s) % chips

    def ag_copy(st, d, hop, q):
        return remote(
            x.at[st, place[slot(d, hop - 1)], 0, some(q)],
            x.at[st, place[slot(d, hop)], 0, some(q)],
            ag_s.at[st, d, hop - 1, q],
            ag_r.at[st, d, hop - 1, q],
            neighbours[d],
        )

    def pf_copy(st, s, q):
        return remote(
            x.at[st, place[s], 0, some(q)],
            x.at[st, place[mirror(s)], 1, some(q)],
            pf_s.at[st, s, q],
            pf_r.at[st, mirror(s), q],
            partner,
        )

    def pc_copy(st, s):
        return remote(
            x.at[st, place[s], 1, :, values],
            pc.at[st, mirror(s)],
            pc_s.at[st, s],
            pc_r.at[st, mirror(s)],
            partner,
        )

    def rs_copy(st, d, hop, q):
        target = slot(d, hop - 1) if (d == 0 or hop > 1) else chips // 2
        return remote(
            x.at[st, place[slot(d, hop)], 0, some(q), values],
            rs.at[st, target, some(q)],
            rs_s.at[st, d, hop - 1, q],
            rs_r.at[st, d, hop - 1, q],
            neighbours[1 - d],
        )

    own = [
        pltpu.make_async_copy(
            hidden_ref.at[st], x.at[st, 0, 0, :, values], load_sem.at[3 + st]
        )
        for st in range(steps)
    ]
    for copy in own:
        copy.start()
    loads = [
        pltpu.make_async_copy(src.at[0], dst, load_sem.at[i])
        for i, (src, dst) in enumerate(((gate_hbm, gate), (up_hbm, up), (down_hbm, down)))
    ]
    for copy in loads:
        copy.start()

    barrier = pltpu.get_barrier_semaphore()
    for target in (*neighbours, partner):
        pl.semaphore_signal(barrier, inc=1, device_id=target, device_id_type=MESH)

    extra = x.shape[4] - width
    lane = lax.broadcasted_iota(jnp.int32, (rows, extra), 1)
    for st in range(steps):
        raw = weights_ref[st]
        normalized = (raw / jnp.sum(raw, axis=0, keepdims=True)).T
        ids = ids_ref[st].T
        dense = jnp.zeros((rows, extra), jnp.float32)
        for k in range(ids.shape[1]):
            label = ids[:, k : k + 1]
            hit = (lane == label) | (lane == label + experts)
            dense = dense + jnp.where(hit, normalized[:, k : k + 1], 0.0)
        high = dense.astype(jnp.bfloat16).astype(jnp.float32)
        low = dense - high
        x[st, 0, 0, :, pl.ds(width, extra)] = jnp.where(lane < experts, high, low).astype(
            jnp.bfloat16
        )
    pl.semaphore_wait(barrier, 3)

    def ag_open(st):
        own[st].wait()
        for q in range(CUTS):
            for d in range(2):
                ag_copy(st, d, 1, q).start()
        for q in range(CUTS):
            pf_copy(st, 0, q).start()

    def ag_event(st, hop, q):
        for d in range(2):
            if hop <= hops[d]:
                ag_copy(st, d, hop, q).wait_recv()
                if hop < hops[d]:
                    ag_copy(st, d, hop + 1, q).start()
                pf_copy(st, slot(d, hop), q).start()

    def total(st, s, received, q):
        value = x[st, place[s], 0, some(q), values].astype(jnp.float32)
        value = value + pc[st, s, some(q)].astype(jnp.float32)
        for index in received:
            value = value + rs[st, index, some(q)].astype(jnp.float32)
        return value.astype(jnp.bfloat16)

    def rs_event(st, age, q):
        for d in range(2):
            hop = hops[d] - age
            if hop >= 1:
                s = slot(d, hop)
                received = []
                if age:
                    rs_copy(st, d, hop + 1, q).wait_recv()
                    received = [s]
                if q == 0:
                    pc_copy(st, mirror(s)).wait_recv()
                x[st, place[s], 0, some(q), values] = total(st, s, received, q)
                rs_copy(st, d, hop, q).start()

    def rs_close(st, q):
        if q == 0:
            pc_copy(st, 0).wait_recv()
        for d in range(2):
            rs_copy(st, d, 1, q).wait_recv()
        out_ref[st, some(q)] = total(st, 0, [0, chips // 2], q)

    group = chips // 2
    block = min(4, group)
    tall = block * 2 * rows
    ff_tile = 256 if inner % 256 == 0 else inner
    out_tile = 512 if width % 512 == 0 else width

    def over_blocks(first, body):
        if group == block:
            body(first, 0)
        else:
            def step(i, carry):
                body(first + i * block, i * tall)
                return carry

            lax.fori_loop(0, group // block, step, 0)

    def gate_up(st, part, tile):
        columns = pl.ds(tile * ff_tile, ff_tile)

        def body(first, row):
            rows_in = x[st, pl.ds(first, block), :, :, values].reshape(tall, width)
            g = jnp.dot(rows_in, gate[:, columns], preferred_element_type=jnp.float32)
            u = jnp.dot(rows_in, up[:, columns], preferred_element_type=jnp.float32)
            mid[pl.ds(row, tall), columns] = (g / (1.0 + jnp.exp(-g)) * u).astype(jnp.bfloat16)

        over_blocks(part * group, body)

    def down_all(st, part):
        for s in order[part * group : (part + 1) * group]:
            for q in range(CUTS):
                pf_copy(st, s, q).wait_send()
                for d in range(2):
                    for hop in range(hops[d]):
                        if slot(d, hop) == s:
                            ag_copy(st, d, hop + 1, q).wait_send()

        def body(first, row):
            marks = x[st, pl.ds(first, block), :, :, pl.ds(width, extra)].reshape(tall, extra)
            spot = lax.broadcasted_iota(jnp.int32, (tall, extra), 1)
            picked = (spot == me) | (spot == me + experts)
            scale = jnp.sum(
                jnp.where(picked, marks.astype(jnp.float32), 0.0), axis=1, keepdims=True
            )
            rows_in = mid[pl.ds(row, tall), :]

            def tile(i, carry):
                columns = pl.ds(pl.multiple_of(i * out_tile, out_tile), out_tile)
                y = jnp.dot(rows_in, down[:, columns], preferred_element_type=jnp.float32)
                y = (y * scale).astype(jnp.bfloat16).reshape(block, 2, rows, out_tile)
                x[st, pl.ds(first, block), :, :, columns] = y
                return carry

            lax.fori_loop(0, width // out_tile, tile, 0)

        over_blocks(part * group, body)
        for s in order[part * group : (part + 1) * group]:
            pc_copy(st, s).start()

    def arrive(st, part):
        for s in order[part * group : (part + 1) * group]:
            for q in range(CUTS):
                pf_copy(st, mirror(s), q).wait_recv()

    def compute(st, part, events):
        tiles = inner // ff_tile
        pieces = tiles + 1
        arrive(st, part)
        taken = 0
        for piece in range(pieces):
            if piece < tiles:
                gate_up(st, part, piece)
            else:
                down_all(st, part)
            until = (piece + 1) * len(events) // pieces
            for event in events[taken:until]:
                event()
            taken = until

    near = group // 2
    call = functools.partial

    def gathers(st, first, last):
        return [
            call(ag_event, st, hop, q) for hop in range(first, last + 1) for q in range(CUTS)
        ]

    def returns(st, first, last):
        return [call(rs_event, st, age, q) for age in range(first, last) for q in range(CUTS)]

    def mixed(one, two):
        keyed = [((i + 1) / len(one), 0, i, e) for i, e in enumerate(one)]
        keyed += [((i + 1) / len(two), 1, i, e) for i, e in enumerate(two)]
        return [entry[3] for entry in sorted(keyed, key=lambda entry: entry[:3])]

    far = hops[0]
    ag_open(0)
    for event in gathers(0, 1, near):
        event()
    for copy in loads:
        copy.wait()
    compute(0, 0, gathers(0, near + 1, far - 1) + [call(ag_open, 1)] + gathers(0, far, far))
    compute(0, 1, gathers(1, 1, near))
    middle = max(1, far // 2)
    for event in returns(0, 0, 1):
        event()
    compute(1, 0, mixed(gathers(1, near + 1, far), returns(0, 1, middle)))
    closing = [call(rs_close, 0, q) for q in range(CUTS)]
    compute(1, 1, returns(0, middle, far))
    for event in returns(1, 0, 1) + closing + returns(1, 1, far):
        event()
    for q in range(CUTS):
        rs_close(1, q)

    for st in range(steps):
        for d in range(2):
            for hop in range(1, hops[d] + 1):
                for q in range(CUTS):
                    rs_copy(st, d, hop, q).wait_send()
        for s in range(chips):
            pc_copy(st, s).wait_send()


def on_device(across, hidden_states, route_ids, route_weights, gate_proj, up_proj, down_proj):
    steps, rows, width = hidden_states.shape
    experts = lax.axis_size("expert")
    inner = gate_proj.shape[2]
    chips = experts // 2
    hops = chips // 2
    extra = -(-2 * experts // LANES) * LANES
    dma = pltpu.SemaphoreType.DMA
    bf16 = jnp.bfloat16
    vmem = pl.BlockSpec(memory_space=pltpu.VMEM)
    hbm = pl.BlockSpec(memory_space=pl.ANY)
    return pl.pallas_call(
        functools.partial(kernel, chips, across),
        out_shape=jax.ShapeDtypeStruct((steps, rows, width), bf16),
        in_specs=[hbm, vmem, vmem, hbm, hbm, hbm],
        out_specs=vmem,
        scratch_shapes=[
            pltpu.VMEM((steps, chips, 2, rows, width + extra), bf16),
            pltpu.VMEM((steps, chips, rows, width), bf16),
            pltpu.VMEM((steps, chips, rows, width), bf16),
            pltpu.VMEM((width, inner), bf16),
            pltpu.VMEM((width, inner), bf16),
            pltpu.VMEM((inner, width), bf16),
            pltpu.VMEM((chips * rows, inner), bf16),
            dma((3 + steps,)),
            dma((steps, 2, hops, CUTS)),
            dma((steps, 2, hops, CUTS)),
            dma((steps, chips, CUTS)),
            dma((steps, chips, CUTS)),
            dma((steps, chips)),
            dma((steps, chips)),
            dma((steps, 2, hops, CUTS)),
            dma((steps, 2, hops, CUTS)),
        ],
        compiler_params=pltpu.CompilerParams(
            collective_id=0, has_side_effects=True, vmem_limit_bytes=64_000_000
        ),
    )(hidden_states, route_ids.swapaxes(1, 2), route_weights.swapaxes(1, 2), gate_proj, up_proj, down_proj)


def solution(mesh):
    across = 2 if mesh.shape["groups"] == 2 else 1
    placed = (
        P(None, ("groups", "expert"), None),
        P(None, ("groups", "expert"), None),
        P(None, ("groups", "expert"), None),
        P("expert", None, None),
        P("expert", None, None),
        P("expert", None, None),
    )
    return jax.shard_map(
        functools.partial(on_device, across),
        mesh=mesh,
        in_specs=placed,
        out_specs=P(None, ("groups", "expert"), None),
        check_vma=False,
    )
```

```python
import functools

import jax
import jax.numpy as jnp
from jax import lax
from jax.experimental import pallas as pl
from jax.experimental.pallas import tpu as pltpu
from jax.sharding import PartitionSpec as P

MESH = pl.DeviceIdType.MESH
LANES = 128
CUTS = 2


def kernel(
    chips,
    across,
    hidden_ref,
    ids_ref,
    weights_ref,
    gate_hbm,
    up_hbm,
    down_hbm,
    out_ref,
    x,
    pc,
    rs,
    gate,
    up,
    down,
    mid,
    load_sem,
    ag_s,
    ag_r,
    pf_s,
    pf_r,
    pc_s,
    pc_r,
    rs_s,
    rs_r,
):
    steps, _, _, rows, _ = x.shape
    width = out_ref.shape[2]
    inner = gate.shape[1]
    experts = 2 * chips
    hops = (chips // 2, chips - 1 - chips // 2)
    along = chips // across

    me = lax.axis_index("expert")
    core = lax.rem(me, 2)
    chip = lax.div(me, 2)
    if across == 2:
        far, deep = lax.rem(chip, 2), lax.div(chip, 2)
        here = (1 - far) * deep + far * (2 * along - 1 - deep)
    else:
        here = chip

    def device_at(position):
        if across == 2:
            far = lax.div(position, along)
            deep = (1 - far) * position + far * (2 * along - 1 - position)
            position = deep * 2 + far
        return {"expert": position * 2 + core}

    sign = 1 - 2 * core
    neighbours = (
        device_at(lax.rem(here + sign + chips, chips)),
        device_at(lax.rem(here - sign + chips, chips)),
    )
    partner = {"expert": chip * 2 + (1 - core)}

    def slot(direction, hop):
        return hop if direction == 0 else (chips - hop) % chips

    order = [0]
    for hop in range(1, chips // 2 + 1):
        order += [slot(d, hop) for d in range(2) if hop <= hops[d]]
    place = {s: i for i, s in enumerate(order)}
    values = pl.ds(0, width)
    cut = rows // CUTS

    def some(q):
        return pl.ds(q * cut, cut)

    def remote(src, dst, send, recv, target):
        return pltpu.make_async_remote_copy(
            src_ref=src,
            dst_ref=dst,
            send_sem=send,
            recv_sem=recv,
            device_id=target,
            device_id_type=MESH,
        )

    def mirror(s):
        return (chips - s) % chips

    def ag_copy(st, d, hop, q):
        return remote(
            x.at[st, place[slot(d, hop - 1)], 0, some(q)],
            x.at[st, place[slot(d, hop)], 0, some(q)],
            ag_s.at[st, d, hop - 1, q],
            ag_r.at[st, d, hop - 1, q],
            neighbours[d],
        )

    def pf_copy(st, s, q):
        return remote(
            x.at[st, place[s], 0, some(q)],
            x.at[st, place[mirror(s)], 1, some(q)],
            pf_s.at[st, s, q],
            pf_r.at[st, mirror(s), q],
            partner,
        )

    def pc_copy(st, s):
        return remote(
            x.at[st, place[s], 1, :, values],
            pc.at[st, mirror(s)],
            pc_s.at[st, s],
            pc_r.at[st, mirror(s)],
            partner,
        )

    def rs_copy(st, d, hop, q):
        target = slot(d, hop - 1) if (d == 0 or hop > 1) else chips // 2
        return remote(
            x.at[st, place[slot(d, hop)], 0, some(q), values],
            rs.at[st, target, some(q)],
            rs_s.at[st, d, hop - 1, q],
            rs_r.at[st, d, hop - 1, q],
            neighbours[1 - d],
        )

    barrier = pltpu.get_barrier_semaphore()
    for target in (*neighbours, partner):
        pl.semaphore_signal(barrier, inc=1, device_id=target, device_id_type=MESH)

    own = [
        pltpu.make_async_copy(
            hidden_ref.at[st], x.at[st, 0, 0, :, values], load_sem.at[3 + st]
        )
        for st in range(steps)
    ]
    for copy in own:
        copy.start()
    loads = [
        pltpu.make_async_copy(src.at[0], dst, load_sem.at[i])
        for i, (src, dst) in enumerate(((gate_hbm, gate), (up_hbm, up), (down_hbm, down)))
    ]
    for copy in loads:
        copy.start()

    extra = x.shape[4] - width
    lane = lax.broadcasted_iota(jnp.int32, (rows, extra), 1)
    for st in range(steps):
        raw = weights_ref[st]
        normalized = (raw / jnp.sum(raw, axis=0, keepdims=True)).T
        ids = ids_ref[st].T
        dense = jnp.zeros((rows, extra), jnp.float32)
        for k in range(ids.shape[1]):
            label = ids[:, k : k + 1]
            hit = (lane == label) | (lane == label + experts)
            dense = dense + jnp.where(hit, normalized[:, k : k + 1], 0.0)
        high = dense.astype(jnp.bfloat16).astype(jnp.float32)
        low = dense - high
        x[st, 0, 0, :, pl.ds(width, extra)] = jnp.where(lane < experts, high, low).astype(
            jnp.bfloat16
        )
    pl.semaphore_wait(barrier, 3)

    def ag_open(st):
        own[st].wait()
        for q in range(CUTS):
            for d in range(2):
                ag_copy(st, d, 1, q).start()
        for q in range(CUTS):
            pf_copy(st, 0, q).start()

    def ag_event(st, hop, q):
        for d in range(2):
            if hop <= hops[d]:
                ag_copy(st, d, hop, q).wait_recv()
                if hop < hops[d]:
                    ag_copy(st, d, hop + 1, q).start()
                pf_copy(st, slot(d, hop), q).start()

    def total(st, s, received, q):
        value = x[st, place[s], 0, some(q), values].astype(jnp.float32)
        value = value + pc[st, s, some(q)].astype(jnp.float32)
        for index in received:
            value = value + rs[st, index, some(q)].astype(jnp.float32)
        return value.astype(jnp.bfloat16)

    def rs_event(st, age, q):
        for d in range(2):
            hop = hops[d] - age
            if hop >= 1:
                s = slot(d, hop)
                received = []
                if age:
                    rs_copy(st, d, hop + 1, q).wait_recv()
                    received = [s]
                if q == 0:
                    pc_copy(st, mirror(s)).wait_recv()
                x[st, place[s], 0, some(q), values] = total(st, s, received, q)
                rs_copy(st, d, hop, q).start()

    def rs_close(st, q):
        if q == 0:
            pc_copy(st, 0).wait_recv()
        for d in range(2):
            rs_copy(st, d, 1, q).wait_recv()
        out_ref[st, some(q)] = total(st, 0, [0, chips // 2], q)

    group = chips // 2
    block = min(4, group)
    tall = block * 2 * rows
    ff_tile = 256 if inner % 256 == 0 else inner
    out_tile = 512 if width % 512 == 0 else width

    def over_blocks(first, body):
        if group == block:
            body(first, 0)
        else:
            def step(i, carry):
                body(first + i * block, i * tall)
                return carry

            lax.fori_loop(0, group // block, step, 0)

    def gate_up(st, part, tile):
        columns = pl.ds(tile * ff_tile, ff_tile)

        def body(first, row):
            rows_in = x[st, pl.ds(first, block), :, :, values].reshape(tall, width)
            g = jnp.dot(rows_in, gate[:, columns], preferred_element_type=jnp.float32)
            u = jnp.dot(rows_in, up[:, columns], preferred_element_type=jnp.float32)
            mid[pl.ds(row, tall), columns] = (g / (1.0 + jnp.exp(-g)) * u).astype(jnp.bfloat16)

        over_blocks(part * group, body)

    def down_all(st, part):
        for s in order[part * group : (part + 1) * group]:
            for q in range(CUTS):
                pf_copy(st, s, q).wait_send()
                for d in range(2):
                    for hop in range(hops[d]):
                        if slot(d, hop) == s:
                            ag_copy(st, d, hop + 1, q).wait_send()

        def body(first, row):
            marks = x[st, pl.ds(first, block), :, :, pl.ds(width, extra)].reshape(tall, extra)
            spot = lax.broadcasted_iota(jnp.int32, (tall, extra), 1)
            picked = (spot == me) | (spot == me + experts)
            scale = jnp.sum(
                jnp.where(picked, marks.astype(jnp.float32), 0.0), axis=1, keepdims=True
            )
            rows_in = mid[pl.ds(row, tall), :]

            def tile(i, carry):
                columns = pl.ds(pl.multiple_of(i * out_tile, out_tile), out_tile)
                y = jnp.dot(rows_in, down[:, columns], preferred_element_type=jnp.float32)
                y = (y * scale).astype(jnp.bfloat16).reshape(block, 2, rows, out_tile)
                x[st, pl.ds(first, block), :, :, columns] = y
                return carry

            lax.fori_loop(0, width // out_tile, tile, 0)

        over_blocks(part * group, body)
        for s in order[part * group : (part + 1) * group]:
            pc_copy(st, s).start()

    def arrive(st, part):
        for s in order[part * group : (part + 1) * group]:
            for q in range(CUTS):
                pf_copy(st, mirror(s), q).wait_recv()

    def compute(st, part, events):
        tiles = inner // ff_tile
        pieces = tiles + 1
        arrive(st, part)
        taken = 0
        for piece in range(pieces):
            if piece < tiles:
                gate_up(st, part, piece)
            else:
                down_all(st, part)
            until = (piece + 1) * len(events) // pieces
            for event in events[taken:until]:
                event()
            taken = until

    near = group // 2
    call = functools.partial

    def gathers(st, first, last):
        return [
            call(ag_event, st, hop, q) for hop in range(first, last + 1) for q in range(CUTS)
        ]

    def returns(st, first, last):
        return [call(rs_event, st, age, q) for age in range(first, last) for q in range(CUTS)]

    far = hops[0]
    first, second = gathers(0, near + 1, far), gathers(1, 1, far)
    half = len(first) // 2
    ag_open(0)
    for event in gathers(0, 1, near):
        event()
    ag_open(1)
    for copy in loads:
        copy.wait()
    compute(0, 0, first[:half] + second[:half] + first[half:])
    compute(0, 1, second[half : 3 * half])
    middle = max(1, far // 2)
    for event in returns(0, 0, 1):
        event()
    compute(1, 0, second[3 * half :] + returns(0, 1, middle))
    compute(1, 1, returns(0, middle, far - 1))
    closing = [call(rs_close, 0, q) for q in range(CUTS)]
    for event in returns(1, 0, 1) + returns(0, far - 1, far) + returns(1, 1, 2):
        event()
    for event in closing + returns(1, 2, far):
        event()
    for q in range(CUTS):
        rs_close(1, q)

    for st in range(steps):
        for d in range(2):
            for hop in range(1, hops[d] + 1):
                for q in range(CUTS):
                    rs_copy(st, d, hop, q).wait_send()
        for s in range(chips):
            pc_copy(st, s).wait_send()


def on_device(across, hidden_states, route_ids, route_weights, gate_proj, up_proj, down_proj):
    steps, rows, width = hidden_states.shape
    experts = lax.axis_size("expert")
    inner = gate_proj.shape[2]
    chips = experts // 2
    hops = chips // 2
    extra = -(-2 * experts // LANES) * LANES
    dma = pltpu.SemaphoreType.DMA
    bf16 = jnp.bfloat16
    vmem = pl.BlockSpec(memory_space=pltpu.VMEM)
    hbm = pl.BlockSpec(memory_space=pl.ANY)
    return pl.pallas_call(
        functools.partial(kernel, chips, across),
        out_shape=jax.ShapeDtypeStruct((steps, rows, width), bf16),
        in_specs=[hbm, vmem, vmem, hbm, hbm, hbm],
        out_specs=vmem,
        scratch_shapes=[
            pltpu.VMEM((steps, chips, 2, rows, width + extra), bf16),
            pltpu.VMEM((steps, chips, rows, width), bf16),
            pltpu.VMEM((steps, chips, rows, width), bf16),
            pltpu.VMEM((width, inner), bf16),
            pltpu.VMEM((width, inner), bf16),
            pltpu.VMEM((inner, width), bf16),
            pltpu.VMEM((chips * rows, inner), bf16),
            dma((3 + steps,)),
            dma((steps, 2, hops, CUTS)),
            dma((steps, 2, hops, CUTS)),
            dma((steps, chips, CUTS)),
            dma((steps, chips, CUTS)),
            dma((steps, chips)),
            dma((steps, chips)),
            dma((steps, 2, hops, CUTS)),
            dma((steps, 2, hops, CUTS)),
        ],
        compiler_params=pltpu.CompilerParams(
            collective_id=0, has_side_effects=True, vmem_limit_bytes=64_000_000
        ),
    )(hidden_states, route_ids.swapaxes(1, 2), route_weights.swapaxes(1, 2), gate_proj, up_proj, down_proj)


def solution(mesh):
    across = 2 if mesh.shape["groups"] == 2 else 1
    placed = (
        P(None, ("groups", "expert"), None),
        P(None, ("groups", "expert"), None),
        P(None, ("groups", "expert"), None),
        P("expert", None, None),
        P("expert", None, None),
        P("expert", None, None),
    )
    return jax.shard_map(
        functools.partial(on_device, across),
        mesh=mesh,
        in_specs=placed,
        out_specs=P(None, ("groups", "expert"), None),
        check_vma=False,
    )
```
